32 devices in a mesh: gx: 8 (over y, x, core), gz: 4 (over z).
Axes of the slice: x: 2, y: 2, z: 4, core: 2. Of those that a mesh axis runs over, the one named last changes fastest.
Arguments:
- adjoint: float32 [5, 32, 256, 512], P(None, 'gx', None, 'gz'), may hold values from -6 to 6
- flow_state: float32 [5, 32, 256, 512], P(None, 'gx', None, 'gz'), may hold values from -6 to 6
- jacobians: float32 [3, 5, 5], replicated, may hold values from -2.5 to 2.5
- metric: float32 [3, 3, 32, 256, 512], P(None, None, 'gx', None, 'gz'), may hold values from -6 to 6
- wing_cells: int32 [32, 256, 512], P('gx', None, 'gz'), may hold values 0 or 1
- modulus: float32 [32, 256, 512], P('gz', 'gx'), may hold values from 0.5 to 2
- stiff_class: int32 [32, 256, 512], P('gz', 'gx'), may hold values from 0 to 7
- fixed_cells: int32 [32, 256, 512], P('gz', 'gx'), may hold values 0 or 1
Outputs:
- displacement: float32 [3, 32, 256, 512], P(None, 'gz', 'gx')
The draws below stay inside these ranges and needn't reach their ends.
All inputs are finite; a program needn't handle non-finite values. No bound on the sum of `wing_cells` or of `fixed_cells` on one device may be relied on, other than what follows from the above.
Results may differ from the reference program's by a relative error of at most 0.0001.
Values sent between devices are 32-bit elements; how exact they have to be, the bound alone decides.
A program may use at most 256 MiB of HBM per device.

```python
import math
import jax
import jax.numpy as jnp
from jax import lax

SWEEPS = 3
NX = 32
NY = 256
NZ = 512


def with_ends(drawn, rng, low, top_value):
    longest = drawn.shape.index(max(drawn.shape))
    spots = []
    for shift in (0, 1):
        where = [jax.random.randint(jax.random.fold_in(rng, axis), (), 0, length) for axis, length in enumerate(drawn.shape)]
        where[longest] = (where[longest] + shift) % drawn.shape[longest]
        spots.append(tuple(where))
    return drawn.at[spots[0]].set(low).at[spots[1]].set(top_value)


def block_scale(stream_key, extent, shards, low, top_value):
    loudness, own = 1.0, jax.random.fold_in(stream_key, 6)
    for position, blocks in shards:
        draws = jnp.exp(jax.random.uniform(jax.random.fold_in(own, position), (blocks,), jnp.float32, low / len(shards), top_value / len(shards)))
        loudness = loudness * jnp.repeat(draws, extent[position] // blocks).reshape([-1 if axis == position else 1 for axis in range(len(extent))])
    return loudness


def gaussian(own_key, shape, scale, limit, shards=(), held_as=jnp.bfloat16):
    level = block_scale(own_key, shape, shards, -0.22, 0.18) if shards else 1.0
    drawn = jax.random.normal(own_key, shape, jnp.float32) * scale * level
    return jnp.minimum(jnp.maximum(drawn, -limit), limit).astype(held_as)


def setup_inputs(seed: int = 0) -> dict:
    keys = jax.random.split(jax.random.key(seed), 9)
    return {
        "adjoint": gaussian(keys[0], (5, NX, NY, NZ), 1.0, 6.0, ((1, 8), (3, 4)), jnp.float32),
        "flow_state": gaussian(keys[1], (5, NX, NY, NZ), 1.0, 6.0, ((1, 8), (3, 4)), jnp.float32),
        "jacobians": gaussian(keys[2], (3, 5, 5), 5 ** -0.5, 2.5, (), jnp.float32),
        "metric": gaussian(keys[3], (3, 3, NX, NY, NZ), 1.0, 6.0, ((2, 8), (4, 4)), jnp.float32),
        "wing_cells": with_ends((jax.random.randint(keys[4], (NX, NY, NZ), 0, 4) < 1).astype(jnp.int32), jax.random.fold_in(keys[4], 1), 0, 1),
        "modulus": jnp.clip(jnp.exp(math.log(2.0) - 1.3862944 * jax.random.uniform(keys[5], (NX, NY, NZ), jnp.float32) ** block_scale(keys[5], (NX, NY, NZ), ((0, 4), (1, 8)), -0.2, 0.2)), 0.5, 2.0),
        "stiff_class": with_ends(jax.random.randint(keys[6], (NX, NY, NZ), 0, 8), jax.random.fold_in(keys[6], 1), 0, 7).astype(jnp.int32),
        "fixed_cells": with_ends((jax.random.randint(keys[7], (NX, NY, NZ), 0, 8) < 1).astype(jnp.int32), jax.random.fold_in(keys[7], 1), 0, 1),
    }


relax_factor = 0.8
mass_term = 0.5
neighbour_offsets = ((0, 1), (0, -1), (1, 1), (1, -1), (2, 1), (2, -1))


def offset_view(array, axis, offset):
    windows = [slice(1, array.shape[array.ndim - 3 + i] - 1) for i in range(3)]
    length = array.shape[array.ndim - 3 + axis]
    windows[axis] = slice(1 + offset, length - 1 + offset)
    leading = (slice(None),) * (array.ndim - 3)
    return array[leading + tuple(windows)]


def flow_terms(extended, jacobians, metric, wing_cells):
    adjoint_ext = extended[:5]
    state_ext = extended[5:]
    state_mid = offset_view(state_ext, 0, 0)
    wing = wing_cells.astype(jnp.float32) * state_mid[4]
    sensitivity = jnp.stack([wing * state_mid[1 + comp] for comp in range(3)])
    for direction in range(3):
        flux_ext = jnp.einsum("kl,lxyz->kxyz", jacobians[direction], state_ext, precision=lax.Precision.HIGHEST)
        adj_lo = offset_view(adjoint_ext, direction, -1)
        adj_mid = offset_view(adjoint_ext, direction, 0)
        adj_hi = offset_view(adjoint_ext, direction, 1)
        flux_lo = offset_view(flux_ext, direction, -1)
        flux_mid = offset_view(flux_ext, direction, 0)
        flux_hi = offset_view(flux_ext, direction, 1)
        face_lower = jnp.sum((adj_mid - adj_lo) * (flux_lo + flux_mid) * 0.5, axis=0)
        face_upper = jnp.sum((adj_hi - adj_mid) * (flux_mid + flux_hi) * 0.5, axis=0)
        sensitivity = sensitivity + metric[direction] * (face_lower - face_upper)[None]
    return sensitivity


def couplings(stiff_ext):
    centre_stiff = offset_view(stiff_ext, 0, 0)
    return [0.5 * (centre_stiff + offset_view(stiff_ext, axis, offset)) for axis, offset in neighbour_offsets]


def diagonal_of(faces):
    total = mass_term + faces[0]
    for face in faces[1:]:
        total = total + face
    return total


def relax_sweep(field, field_ext, sensitivity, diag, free, faces):
    coupled = faces[0] * offset_view(field_ext, 0, 1)
    for index in range(1, 6):
        axis, offset = neighbour_offsets[index]
        coupled = coupled + faces[index] * offset_view(field_ext, axis, offset)
    return free * (field + relax_factor * (sensitivity - (diag * field - coupled)) / diag)


def reference(adjoint, flow_state, jacobians, metric, wing_cells, modulus, stiff_class, fixed_cells):
    stacked = jnp.concatenate([adjoint, flow_state], axis=0)
    extended = jnp.pad(stacked, ((0, 0), (1, 1), (1, 1), (1, 1)))
    sensitivity = flow_terms(extended, jacobians, metric, wing_cells)
    stiffness = modulus * jnp.exp2(-0.5 * stiff_class.astype(jnp.float32))
    free = 1.0 - fixed_cells.astype(jnp.float32)
    faces = couplings(jnp.pad(stiffness, 1))
    diag = diagonal_of(faces)
    field = jnp.zeros_like(sensitivity)
    for sweep in range(SWEEPS):
        field_ext = jnp.pad(field, ((0, 0), (1, 1), (1, 1), (1, 1)))
        field = relax_sweep(field, field_ext, sensitivity, diag, free, faces)
    return field
```

```python
import functools

import jax
import jax.numpy as jnp
from jax import lax
from jax.experimental import pallas as pl
from jax.experimental.pallas import tpu as pltpu
from jax.sharding import PartitionSpec as P

SWEEPS = 3
RELAX = 0.8
MASS = 0.5
PAD = 8
LANES = 128
MESH = pl.DeviceIdType.MESH
F32 = jnp.float32


def face_of(jac, d, lo_a, lo_s, hi_a, hi_s):
    both = [lo_s[l] + hi_s[l] for l in range(5)]
    total = None
    for k in range(5):
        flux = jac[d, k, 0] * both[0]
        for l in range(1, 5):
            flux = flux + jac[d, k, l] * both[l]
        term = (hi_a[k] - lo_a[k]) * flux
        total = term if total is None else total + term
    return total * 0.5


def kernel(nx, nz, jac, adj_h, st_h, met_h, wing_h, mod_h, cls_h, fix_h, out,
           adj, st, met, wing, mod, cls, fix,
           halo, zpack, zrecv, zface, fx, xface, sens, mid, recv,
           stiff, srow, srow_in, wgt, coup, field_a, field_b, frow, frow_in,
           load_sem, xh_s, xh_r, zh_s, zh_r, xf_s, xf_r,
           s1, r1, s2, r2, sp_s, sp_r, sr_s, sr_r, fp_s, fp_r, fr_s, fr_r):
    a, b = lax.axis_index("gx"), lax.axis_index("gz")
    per = nx // nz
    ny = wing.shape[1]
    half_y = ny // 2
    xt, yt, span = mod.shape
    lane = lax.broadcasted_iota(jnp.int32, (yt, LANES), 1)
    has_lo, has_hi = a > 0, a < nx - 1
    has_dn, has_up = b > 0, b < nz - 1

    loads = [
        pltpu.make_async_copy(adj_h, adj.at[:, :, pl.ds(PAD, ny), :], load_sem.at[0]),
        pltpu.make_async_copy(st_h, st.at[:, :, pl.ds(PAD, ny), :], load_sem.at[1]),
        pltpu.make_async_copy(mod_h, mod, load_sem.at[2]),
        pltpu.make_async_copy(cls_h, cls, load_sem.at[3]),
        pltpu.make_async_copy(fix_h, fix, load_sem.at[4]),
        pltpu.make_async_copy(met_h, met, load_sem.at[5]),
        pltpu.make_async_copy(wing_h, wing, load_sem.at[6]),
    ]
    for load in loads:
        load.start()

    for ref in (adj, st):
        for k in range(5):
            for x in range(4):
                ref[k, x, 0:PAD, :] = jnp.zeros((PAD, LANES), F32)
                ref[k, x, PAD + ny:, :] = jnp.zeros((PAD, LANES), F32)

    def zero(ref):
        ref[...] = jnp.zeros(ref.shape, F32)

    def zero_planes(side, z):
        stiff[z, PAD:PAD + yt, :] = jnp.zeros((yt, span), F32)
        for c in range(3):
            for f in (field_a, field_b):
                f[c, z, PAD:PAD + yt, :] = jnp.zeros((yt, span), F32)

    @pl.when(jnp.logical_not(has_lo))
    def _():
        zero(halo.at[0])
        zero(srow_in.at[0])
        zero(frow_in.at[0, 0])
        zero(frow_in.at[1, 0])

    @pl.when(jnp.logical_not(has_hi))
    def _():
        zero(halo.at[1])
        zero(srow_in.at[1])
        zero(frow_in.at[0, 1])
        zero(frow_in.at[1, 1])

    @pl.when(jnp.logical_not(has_dn))
    def _():
        zero(zrecv.at[0])
        zero_planes(0, 0)

    @pl.when(jnp.logical_not(has_up))
    def _():
        zero(zrecv.at[1])
        zero_planes(1, xt + 1)

    bar = pltpu.get_barrier_semaphore()
    for t in range(1, nx):
        pl.semaphore_signal(bar, inc=1, device_id=((a + t) % nx, b), device_id_type=MESH)
    for t in range(1, nz):
        pl.semaphore_signal(bar, inc=1, device_id=(a, (b + t) % nz), device_id_type=MESH)
    pl.semaphore_wait(bar, nx + nz - 2)

    def remote(src, dst, send, rcv, dev):
        return pltpu.make_async_remote_copy(
            src_ref=src, dst_ref=dst, send_sem=send, recv_sem=rcv,
            device_id=dev, device_id_type=MESH)

    lower, upper = (jnp.maximum(a - 1, 0), b), (jnp.minimum(a + 1, nx - 1), b)
    below, above = (a, jnp.maximum(b - 1, 0)), (a, jnp.minimum(b + 1, nz - 1))
    first, second = pl.ds(0, half_y), pl.ds(half_y, half_y)

    to_upper = [remote(src.at[:, 3, first, :], halo.at[0, i], xh_s.at[0, i], xh_r.at[0, i], upper)
                for i, src in enumerate((adj_h, st_h))]
    to_lower = [remote(src.at[:, 0, second, :], halo.at[1, i], xh_s.at[1, i], xh_r.at[1, i], lower)
                for i, src in enumerate((adj_h, st_h))]

    def start_if(cond, copies):
        @pl.when(cond)
        def _():
            for copy in copies:
                copy.start()

    def exchange_wait(cond_send, sends, cond_recv, recvs):
        @pl.when(cond_send)
        def _():
            for copy in sends:
                copy.wait_send()

        @pl.when(cond_recv)
        def _():
            for copy in recvs:
                copy.wait_recv()

    start_if(has_hi, to_upper)
    start_if(has_lo, to_lower)

    loads[0].wait()
    loads[1].wait()

    def pack_rows(n, carry):
        y0 = pl.multiple_of(n * yt, yt)
        acc = jnp.zeros((yt, LANES), F32)
        for which, ref in enumerate((adj, st)):
            for k in range(5):
                for x in range(4):
                    index = which * 20 + k * 4 + x
                    turned = pltpu.roll(ref[k, x, pl.ds(y0 + PAD, yt), :], 2 * index + 1, 1)
                    acc = jnp.where(lane // 2 == index, turned, acc)
        zpack[pl.ds(y0, yt), :] = acc
        return carry

    lax.fori_loop(0, ny // yt, pack_rows, 0)

    loads[2].wait()
    loads[3].wait()
    loads[4].wait()

    def stiff_plane(x, carry):
        value = mod[x] * jnp.exp2(-0.5 * cls[x].astype(F32))
        stiff[x + 1, PAD:PAD + yt, :] = value
        srow[0, pl.ds(x, 1), :] = value[0:1]
        srow[1, pl.ds(x, 1), :] = value[yt - 1:yt]
        return carry

    lax.fori_loop(0, xt, stiff_plane, 0)

    z_up = [remote(zpack, zrecv.at[0], zh_s.at[0], zh_r.at[0], above)]
    z_dn = [remote(zpack, zrecv.at[1], zh_s.at[1], zh_r.at[1], below)]
    start_if(has_up, z_up)
    start_if(has_dn, z_dn)
    rows = pl.ds(PAD, yt)
    sp_up = [remote(stiff.at[xt, rows, :], stiff.at[0, rows, :], sp_s.at[0], sp_r.at[0], above)]
    sp_dn = [remote(stiff.at[1, rows, :], stiff.at[xt + 1, rows, :], sp_s.at[1], sp_r.at[1], below)]
    sr_up = [remote(srow.at[1], srow_in.at[0], sr_s.at[0], sr_r.at[0], upper)]
    sr_lo = [remote(srow.at[0], srow_in.at[1], sr_s.at[1], sr_r.at[1], lower)]
    loads[5].wait()
    loads[6].wait()

    exchange_wait(has_up, z_up, has_dn, z_up)
    exchange_wait(has_dn, z_dn, has_up, z_dn)

    def zface_rows(n, carry):
        y0 = pl.multiple_of(n * yt, yt)
        mine = zpack[pl.ds(y0, yt), :]
        odd = lane % 2 == 1
        other = jnp.where(odd, pltpu.roll(zrecv[0, pl.ds(y0, yt), :], 1, 1),
                          pltpu.roll(zrecv[1, pl.ds(y0, yt), :], LANES - 1, 1))
        diff, both = mine - other, mine + other
        total = None
        states = [pltpu.roll(both, LANES - 40 - 8 * l, 1) for l in range(5)]
        for k in range(5):
            flux = jac[2, k, 0] * states[0]
            for l in range(1, 5):
                flux = flux + jac[2, k, l] * states[l]
            part = diff if k == 0 else pltpu.roll(diff, LANES - 8 * k, 1)
            total = part * flux if total is None else total + part * flux
        zface[pl.ds(y0, yt), :] = jnp.where(odd, 0.5 * total, -0.5 * total)
        return carry

    lax.fori_loop(0, ny // yt, zface_rows, 0)

    def cells(x, y0):
        ds = pl.ds(y0 + PAD, yt)
        return [adj[k, x, ds, :] for k in range(5)], [st[k, x, ds, :] for k in range(5)]

    def store_sens(half, i, x, y0, diff0):
        wide = yt + 8
        low, high = pl.ds(y0, wide), pl.ds(y0 + 1, wide)
        fy = face_of(jac, 1, [adj[k, x, low, :] for k in range(5)], [st[k, x, low, :] for k in range(5)],
                     [adj[k, x, high, :] for k in range(5)], [st[k, x, high, :] for k in range(5)])
        diff1 = fy[7:7 + yt] - fy[8:8 + yt]
        av, sv = cells(x, y0)
        fz = face_of(jac, 2, av, sv, [pltpu.roll(v, LANES - 1, 1) for v in av],
                     [pltpu.roll(v, LANES - 1, 1) for v in sv])
        edge = zface[pl.ds(y0, yt), :]
        z_hi = jnp.where(lane == LANES - 1, pltpu.roll(edge, LANES - 1 - 2 * x, 1), fz)
        z_lo = jnp.where(lane == 0, pltpu.roll(edge, LANES - 1 - 2 * x, 1), pltpu.roll(fz, 1, 1))
        diff2 = z_lo - z_hi
        ys = pl.ds(y0, yt)
        scaled = wing[x, ys, :].astype(F32) * sv[4]
        for c in range(3):
            value = scaled * sv[1 + c]
            value = value + met[0, c, x, ys, :] * diff0
            value = value + met[1, c, x, ys, :] * diff1
            value = value + met[2, c, x, ys, :] * diff2
            sens[half, i, c, ys, :] = value

    def chunk_of(t):
        return (a + 2 * nx - per * b - t) % nx

    def phase1(half, j):
        return remote(sens.at[half, :, :, pl.ds(pl.multiple_of(j * yt, yt), yt), :],
                      mid.at[half, a], s1.at[half, j], r1.at[half, a], (j, b))

    def own_chunk(half):
        return pltpu.make_async_copy(
            sens.at[half, :, :, pl.ds(pl.multiple_of(a * yt, yt), yt), :],
            mid.at[half, a], r1.at[half, a])

    def send_chunk(half, t):
        j = chunk_of(t)

        @pl.when(j != a)
        def _():
            phase1(half, j).start()

        @pl.when(j == a)
        def _():
            own_chunk(half).start()

    def slot(half, f, z):
        return recv.at[half, f % per, :, :, :, pl.ds(pl.multiple_of(z * LANES, LANES), LANES)]

    def phase2(half, f):
        return remote(mid.at[half, f], slot(half, f, b), s2.at[half, f], r2.at[half, f % per, b],
                      (a, f // per))

    def relay(half):
        def step(t, carry):
            f = (a + per * b + t) % nx
            remote(mid.at[half, f], mid.at[half, f], s1.at[half, f], r1.at[half, f], (f, b)).wait_recv()

            @pl.when(f // per != b)
            def _():
                phase2(half, f).start()

            @pl.when(f // per == b)
            def _():
                pltpu.make_async_copy(mid.at[half, f], slot(half, f, b), r2.at[half, f % per, b]).start()
            return carry

        lax.fori_loop(0, nx, step, 0)

    def make_half(half, compute):
        def step(t, carry):
            compute(pl.multiple_of(chunk_of(t) * yt, yt))

            @pl.when(t > 0)
            def _():
                send_chunk(half, t - 1)
            return carry

        lax.fori_loop(0, nx, step, 0)
        start_if(has_up, sp_up if half == 0 else [])
        start_if(has_dn, sp_dn if half == 0 else [])
        start_if(has_hi, sr_up if half == 0 else [])
        start_if(has_lo, sr_lo if half == 0 else [])
        send_chunk(half, nx - 1)

    def inner_planes(y0):
        for x in range(3):
            la, ls = cells(x, y0)
            ha, hs = cells(x + 1, y0)
            fx[x, pl.ds(y0, yt), :] = face_of(jac, 0, la, ls, ha, hs)
        for i, x in enumerate((1, 2)):
            store_sens(0, i, x, y0, fx[x - 1, pl.ds(y0, yt), :] - fx[x, pl.ds(y0, yt), :])

    make_half(0, inner_planes)
    relay(0)

    exchange_wait(has_hi, to_upper, has_lo, to_upper)
    exchange_wait(has_lo, to_lower, has_hi, to_lower)

    def bottom_rows(base):
        def step(n, carry):
            h0 = pl.multiple_of(n * yt, yt)
            ha, hs = cells(0, pl.multiple_of(h0 + base, yt))
            la = [halo[0, 0, k, pl.ds(h0, yt), :] for k in range(5)]
            ls = [halo[0, 1, k, pl.ds(h0, yt), :] for k in range(5)]
            xface[0, pl.ds(pl.multiple_of(h0 + base, yt), yt), :] = face_of(jac, 0, la, ls, ha, hs)
            return carry
        lax.fori_loop(0, half_y // yt, step, 0)

    def top_rows(base):
        def step(n, carry):
            h0 = pl.multiple_of(n * yt, yt)
            la, ls = cells(3, pl.multiple_of(h0 + base, yt))
            ha = [halo[1, 0, k, pl.ds(h0, yt), :] for k in range(5)]
            hs = [halo[1, 1, k, pl.ds(h0, yt), :] for k in range(5)]
            xface[1, pl.ds(pl.multiple_of(h0 + base, yt), yt), :] = face_of(jac, 0, la, ls, ha, hs)
            return carry
        lax.fori_loop(0, half_y // yt, step, 0)

    bottom_rows(0)
    top_rows(half_y)
    xf_lo = [remote(xface.at[0, first, :], xface.at[1, first, :], xf_s.at[0], xf_r.at[0], lower)]
    xf_up = [remote(xface.at[1, second, :], xface.at[0, second, :], xf_s.at[1], xf_r.at[1], upper)]
    start_if(has_lo, xf_lo)
    start_if(has_hi, xf_up)

    @pl.when(jnp.logical_not(has_lo))
    def _():
        bottom_rows(half_y)

    @pl.when(jnp.logical_not(has_hi))
    def _():
        top_rows(0)

    exchange_wait(has_lo, xf_lo, has_hi, xf_lo)
    exchange_wait(has_hi, xf_up, has_lo, xf_up)

    def outer_planes(y0):
        ys = pl.ds(y0, yt)
        store_sens(1, 0, 0, y0, xface[0, ys, :] - fx[0, ys, :])
        store_sens(1, 1, 3, y0, fx[2, ys, :] - xface[1, ys, :])

    make_half(1, outer_planes)

    exchange_wait(has_up, sp_up, has_dn, sp_up)
    exchange_wait(has_dn, sp_dn, has_up, sp_dn)
    exchange_wait(has_hi, sr_up, has_lo, sr_up)
    exchange_wait(has_lo, sr_lo, has_hi, sr_lo)
    relay(1)

    def put_rows(dst, src, side_row):
        dst[side_row:side_row + 1, :] = src

    def coup_plane(x, carry):
        stiff.at[x + 1][PAD - 1:PAD, :] = srow_in[0, pl.ds(x, 1), :]
        stiff.at[x + 1][PAD + yt:PAD + yt + 1, :] = srow_in[1, pl.ds(x, 1), :]
        zl = lax.broadcasted_iota(jnp.int32, (yt, span), 1)
        mid_s = stiff[x + 1, PAD:PAD + yt, :]
        around = [
            stiff[x + 2, PAD:PAD + yt, :],
            stiff[x, PAD:PAD + yt, :],
            stiff[x + 1, PAD + 1:PAD + 1 + yt, :],
            stiff[x + 1, PAD - 1:PAD - 1 + yt, :],
            jnp.where(zl == span - 1, 0.0, pltpu.roll(mid_s, span - 1, 1)),
            jnp.where(zl == 0, 0.0, pltpu.roll(mid_s, 1, 1)),
        ]
        faces = [0.5 * (mid_s + s) for s in around]
        diag = MASS + faces[0]
        for face in faces[1:]:
            diag = diag + face
        free = jnp.where(fix[x] == 0, 1.0, 0.0)
        weight = free * (RELAX / diag)
        wgt[x] = weight
        for n in range(4):
            coup[n, x] = weight * faces[n]
        coup[4, x] = jnp.where(zl == span - 1, 0.0, weight * faces[4])
        coup[5, x] = jnp.where(zl == 0, 0.0, weight * faces[5])
        return carry

    lax.fori_loop(0, xt, coup_plane, 0)

    def arrived(half):
        for h in range(per):
            for z in range(nz):
                dst = slot(half, h, z)
                remote(dst, dst, s2.at[half, 0], r2.at[half, h, z], (a, z)).wait_recv()

    arrived(0)
    arrived(1)

    def put_field(n, c, x, dst, value):
        dst[c, x + 1, PAD:PAD + yt, :] = value
        frow[n, 0, c, pl.ds(x, 1), :] = value[0:1]
        frow[n, 1, c, pl.ds(x, 1), :] = value[yt - 1:yt]

    def first_sweep(h, carry):
        for xl, (half, i) in enumerate(((1, 0), (0, 0), (0, 1), (1, 1))):
            x = h * 4 + xl
            for c in range(3):
                put_field(0, c, x, field_a, wgt[x] * recv[half, h, i, c])
        return carry

    lax.fori_loop(0, per, first_sweep, 0)

    def exchange_field(n, field):
        p_up = [remote(field.at[:, xt, rows, :], field.at[:, 0, rows, :], fp_s.at[n, 0], fp_r.at[n, 0], above)]
        p_dn = [remote(field.at[:, 1, rows, :], field.at[:, xt + 1, rows, :], fp_s.at[n, 1], fp_r.at[n, 1], below)]
        r_up = [remote(frow.at[n, 1], frow_in.at[n, 0], fr_s.at[n, 0], fr_r.at[n, 0], upper)]
        r_lo = [remote(frow.at[n, 0], frow_in.at[n, 1], fr_s.at[n, 1], fr_r.at[n, 1], lower)]
        start_if(has_up, p_up)
        start_if(has_dn, p_dn)
        start_if(has_hi, r_up)
        start_if(has_lo, r_lo)
        return p_up, p_dn, r_up, r_lo

    def relaxed(n, field, x, store):
        for c in range(3):
            field.at[c, x + 1][PAD - 1:PAD, :] = frow_in[n, 0, c, pl.ds(x, 1), :]
            field.at[c, x + 1][PAD + yt:PAD + yt + 1, :] = frow_in[n, 1, c, pl.ds(x, 1), :]
            here = field[c, x + 1, PAD:PAD + yt, :]
            total = coup[0, x] * field[c, x + 2, PAD:PAD + yt, :]
            total = total + coup[1, x] * field[c, x, PAD:PAD + yt, :]
            total = total + coup[2, x] * field[c, x + 1, PAD + 1:PAD + 1 + yt, :]
            total = total + coup[3, x] * field[c, x + 1, PAD - 1:PAD - 1 + yt, :]
            total = total + coup[4, x] * pltpu.roll(here, span - 1, 1)
            total = total + coup[5, x] * pltpu.roll(here, 1, 1)
            start = here if n == 0 else field_a[c, x + 1, PAD:PAD + yt, :]
            store(c, x, (1.0 - RELAX) * here + start + total)

    def sweep(n, field, store):
        p_up, p_dn, r_up, r_lo = exchange_field(n, field)
        exchange_wait(has_hi, r_up, has_lo, r_up)
        exchange_wait(has_lo, r_lo, has_hi, r_lo)

        def step(x, carry):
            relaxed(n, field, x, store)
            return carry

        lax.fori_loop(1, xt - 1, step, 0)
        exchange_wait(has_up, p_up, has_dn, p_up)
        exchange_wait(has_dn, p_dn, has_up, p_dn)
        relaxed(n, field, 0, store)
        relaxed(n, field, xt - 1, store)

    def store_last(c, x, value):
        out[c, x] = value

    sweep(0, field_a, lambda c, x, value: put_field(1, c, x, field_b, value))
    sweep(1, field_b, store_last)

    for half in range(2):
        def drain(t, carry, half=half):
            @pl.when(t != a)
            def _():
                phase1(half, t).wait_send()

            @pl.when(t // per != b)
            def _():
                phase2(half, t).wait_send()
            return carry

        lax.fori_loop(0, nx, drain, 0)


def shards(nx, nz, adjoint, flow_state, jacobians, metric, wing_cells, modulus, stiff_class, fixed_cells):
    ny = adjoint.shape[2]
    xt, yt, span = modulus.shape
    per = nx // nz
    V, D = pltpu.VMEM, pltpu.SemaphoreType.DMA
    anywhere = pl.BlockSpec(memory_space=pl.ANY)
    scratch = [
        V((5, 4, ny + 2 * PAD, LANES), F32),
        V((5, 4, ny + 2 * PAD, LANES), F32),
        V(metric.shape, F32),
        V(wing_cells.shape, jnp.int32),
        V(modulus.shape, F32),
        V(modulus.shape, jnp.int32),
        V(modulus.shape, jnp.int32),
        V((2, 2, 5, ny // 2, LANES), F32),
        V((ny, LANES), F32),
        V((2, ny, LANES), F32),
        V((ny, LANES), F32),
        V((3, ny, LANES), F32),
        V((2, ny, LANES), F32),
        V((2, 2, 3, ny, LANES), F32),
        V((2, nx, 2, 3, yt, LANES), F32),
        V((2, per, 2, 3, yt, span), F32),
        V((xt + 2, yt + 2 * PAD, span), F32),
        V((2, xt, span), F32),
        V((2, xt, span), F32),
        V((xt, yt, span), F32),
        V((6, xt, yt, span), F32),
        V((3, xt + 2, yt + 2 * PAD, span), F32),
        V((3, xt + 2, yt + 2 * PAD, span), F32),
        V((2, 2, 3, xt, span), F32),
        V((2, 2, 3, xt, span), F32),
        D((7,)), D((2, 2)), D((2, 2)), D((2,)), D((2,)), D((2,)), D((2,)),
        D((2, nx)), D((2, nx)), D((2, nx)), D((2, per, nz)),
        D((2,)), D((2,)), D((2,)), D((2,)),
        D((2, 2)), D((2, 2)), D((2, 2)), D((2, 2)),
    ]
    return pl.pallas_call(
        functools.partial(kernel, nx, nz),
        out_shape=jax.ShapeDtypeStruct((3, xt, yt, span), F32),
        in_specs=[pl.BlockSpec(memory_space=pltpu.SMEM)] + [anywhere] * 7,
        out_specs=pl.BlockSpec(memory_space=pltpu.VMEM),
        scratch_shapes=scratch,
        compiler_params=pltpu.CompilerParams(
            collective_id=0, has_side_effects=True, vmem_limit_bytes=63 * 1024 * 1024),
        name="adjoint_step",
    )(jacobians, adjoint, flow_state, metric, wing_cells, modulus, stiff_class, fixed_cells)


def solution(mesh):
    return jax.shard_map(
        functools.partial(shards, mesh.shape["gx"], mesh.shape["gz"]),
        mesh=mesh,
        in_specs=(
            P(None, "gx", None, "gz"),
            P(None, "gx", None, "gz"),
            P(),
            P(None, None, "gx", None, "gz"),
            P("gx", None, "gz"),
            P("gz", "gx", None),
            P("gz", "gx", None),
            P("gz", "gx", None),
        ),
        out_specs=P(None, "gz", "gx", None),
        check_vma=False,
    )
```

```python
import functools

import jax
import jax.numpy as jnp
from jax import lax
from jax.experimental import pallas as pl
from jax.experimental.pallas import tpu as pltpu
from jax.sharding import PartitionSpec as P

SWEEPS = 3
RELAX = 0.8
MASS = 0.5
PAD = 8
LANES = 128
MESH = pl.DeviceIdType.MESH
F32 = jnp.float32


def face_of(jac, d, lo_a, lo_s, hi_a, hi_s):
    both = [lo_s[l] + hi_s[l] for l in range(5)]
    total = None
    for k in range(5):
        flux = jac[d, k, 0] * both[0]
        for l in range(1, 5):
            flux = flux + jac[d, k, l] * both[l]
        term = (hi_a[k] - lo_a[k]) * flux
        total = term if total is None else total + term
    return total * 0.5


def kernel(nx, nz, jac, adj_h, st_h, met_h, wing_h, mod_h, cls_h, fix_h, out,
           adj, st, met, wing, mod, cls, fix,
           halo, zpack, zrecv, zface, fx, xface, sens, mid, recv,
           stiff, srow, srow_in, wgt, coup, field_a, field_b, frow, frow_in,
           load_sem, xh_s, xh_r, zh_s, zh_r, xf_s, xf_r,
           s1, r1, s2, r2, sp_s, sp_r, sr_s, sr_r, fp_s, fp_r, fr_s, fr_r):
    a, b = lax.axis_index("gx"), lax.axis_index("gz")
    per = nx // nz
    ny = wing.shape[1]
    half_y = ny // 2
    xt, yt, span = mod.shape
    lane = lax.broadcasted_iota(jnp.int32, (yt, LANES), 1)
    has_lo, has_hi = a > 0, a < nx - 1
    has_dn, has_up = b > 0, b < nz - 1

    loads = [
        pltpu.make_async_copy(adj_h, adj.at[:, :, pl.ds(PAD, ny), :], load_sem.at[0]),
        pltpu.make_async_copy(st_h, st.at[:, :, pl.ds(PAD, ny), :], load_sem.at[1]),
        pltpu.make_async_copy(mod_h, mod, load_sem.at[2]),
        pltpu.make_async_copy(cls_h, cls, load_sem.at[3]),
        pltpu.make_async_copy(fix_h, fix, load_sem.at[4]),
        pltpu.make_async_copy(met_h, met, load_sem.at[5]),
        pltpu.make_async_copy(wing_h, wing, load_sem.at[6]),
    ]
    for load in loads:
        load.start()

    for ref in (adj, st):
        for k in range(5):
            for x in range(4):
                ref[k, x, 0:PAD, :] = jnp.zeros((PAD, LANES), F32)
                ref[k, x, PAD + ny:, :] = jnp.zeros((PAD, LANES), F32)

    def zero(ref):
        ref[...] = jnp.zeros(ref.shape, F32)

    def zero_planes(side, z):
        stiff[z, PAD:PAD + yt, :] = jnp.zeros((yt, span), F32)
        for c in range(3):
            for f in (field_a, field_b):
                f[c, z, PAD:PAD + yt, :] = jnp.zeros((yt, span), F32)

    @pl.when(jnp.logical_not(has_lo))
    def _():
        zero(halo.at[0])
        zero(srow_in.at[0])
        zero(frow_in.at[0, 0])
        zero(frow_in.at[1, 0])

    @pl.when(jnp.logical_not(has_hi))
    def _():
        zero(halo.at[1])
        zero(srow_in.at[1])
        zero(frow_in.at[0, 1])
        zero(frow_in.at[1, 1])

    @pl.when(jnp.logical_not(has_dn))
    def _():
        zero(zrecv.at[0])
        zero_planes(0, 0)

    @pl.when(jnp.logical_not(has_up))
    def _():
        zero(zrecv.at[1])
        zero_planes(1, xt + 1)

    bar = pltpu.get_barrier_semaphore()
    for t in range(1, nx):
        pl.semaphore_signal(bar, inc=1, device_id=((a + t) % nx, b), device_id_type=MESH)
    for t in range(1, nz):
        pl.semaphore_signal(bar, inc=1, device_id=(a, (b + t) % nz), device_id_type=MESH)
    pl.semaphore_wait(bar, nx + nz - 2)

    def remote(src, dst, send, rcv, dev):
        return pltpu.make_async_remote_copy(
            src_ref=src, dst_ref=dst, send_sem=send, recv_sem=rcv,
            device_id=dev, device_id_type=MESH)

    lower, upper = (jnp.maximum(a - 1, 0), b), (jnp.minimum(a + 1, nx - 1), b)
    below, above = (a, jnp.maximum(b - 1, 0)), (a, jnp.minimum(b + 1, nz - 1))
    first, second = pl.ds(0, half_y), pl.ds(half_y, half_y)

    to_upper = [remote(src.at[:, 3, first, :], halo.at[0, i], xh_s.at[0, i], xh_r.at[0, i], upper)
                for i, src in enumerate((adj_h, st_h))]
    to_lower = [remote(src.at[:, 0, second, :], halo.at[1, i], xh_s.at[1, i], xh_r.at[1, i], lower)
                for i, src in enumerate((adj_h, st_h))]

    def start_if(cond, copies):
        @pl.when(cond)
        def _():
            for copy in copies:
                copy.start()

    def exchange_wait(cond_send, sends, cond_recv, recvs):
        @pl.when(cond_send)
        def _():
            for copy in sends:
                copy.wait_send()

        @pl.when(cond_recv)
        def _():
            for copy in recvs:
                copy.wait_recv()

    start_if(has_hi, to_upper)
    start_if(has_lo, to_lower)

    loads[0].wait()
    loads[1].wait()

    def pack_rows(n, carry):
        y0 = pl.multiple_of(n * yt, yt)
        acc = jnp.zeros((yt, LANES), F32)
        for which, ref in enumerate((adj, st)):
            for k in range(5):
                for x in range(4):
                    index = which * 20 + k * 4 + x
                    turned = pltpu.roll(ref[k, x, pl.ds(y0 + PAD, yt), :], 2 * index + 1, 1)
                    acc = jnp.where(lane // 2 == index, turned, acc)
        zpack[pl.ds(y0, yt), :] = acc
        return carry

    lax.fori_loop(0, ny // yt, pack_rows, 0)

    loads[2].wait()
    loads[3].wait()
    loads[4].wait()

    def stiff_plane(x, carry):
        value = mod[x] * jnp.exp2(-0.5 * cls[x].astype(F32))
        stiff[x + 1, PAD:PAD + yt, :] = value
        srow[0, pl.ds(x, 1), :] = value[0:1]
        srow[1, pl.ds(x, 1), :] = value[yt - 1:yt]
        return carry

    lax.fori_loop(0, xt, stiff_plane, 0)

    z_up = [remote(zpack, zrecv.at[0], zh_s.at[0], zh_r.at[0], above)]
    z_dn = [remote(zpack, zrecv.at[1], zh_s.at[1], zh_r.at[1], below)]
    start_if(has_up, z_up)
    start_if(has_dn, z_dn)
    rows = pl.ds(PAD, yt)
    sp_up = [remote(stiff.at[xt, rows, :], stiff.at[0, rows, :], sp_s.at[0], sp_r.at[0], above)]
    sp_dn = [remote(stiff.at[1, rows, :], stiff.at[xt + 1, rows, :], sp_s.at[1], sp_r.at[1], below)]
    sr_up = [remote(srow.at[1], srow_in.at[0], sr_s.at[0], sr_r.at[0], upper)]
    sr_lo = [remote(srow.at[0], srow_in.at[1], sr_s.at[1], sr_r.at[1], lower)]
    def cells(x, y0):
        ds = pl.ds(y0 + PAD, yt)
        return [adj[k, x, ds, :] for k in range(5)], [st[k, x, ds, :] for k in range(5)]

    def inner_faces(n, carry):
        y0 = pl.multiple_of(n * yt, yt)
        for x in range(3):
            la, ls = cells(x, y0)
            ha, hs = cells(x + 1, y0)
            fx[x, pl.ds(y0, yt), :] = face_of(jac, 0, la, ls, ha, hs)
        return carry

    lax.fori_loop(0, ny // yt, inner_faces, 0)
    loads[5].wait()
    loads[6].wait()

    exchange_wait(has_up, z_up, has_dn, z_up)
    exchange_wait(has_dn, z_dn, has_up, z_dn)

    def zface_rows(n, carry):
        y0 = pl.multiple_of(n * yt, yt)
        mine = zpack[pl.ds(y0, yt), :]
        odd = lane % 2 == 1
        other = jnp.where(odd, pltpu.roll(zrecv[0, pl.ds(y0, yt), :], 1, 1),
                          pltpu.roll(zrecv[1, pl.ds(y0, yt), :], LANES - 1, 1))
        diff, both = mine - other, mine + other
        total = None
        states = [pltpu.roll(both, LANES - 40 - 8 * l, 1) for l in range(5)]
        for k in range(5):
            flux = jac[2, k, 0] * states[0]
            for l in range(1, 5):
                flux = flux + jac[2, k, l] * states[l]
            part = diff if k == 0 else pltpu.roll(diff, LANES - 8 * k, 1)
            total = part * flux if total is None else total + part * flux
        zface[pl.ds(y0, yt), :] = jnp.where(odd, 0.5 * total, -0.5 * total)
        return carry

    lax.fori_loop(0, ny // yt, zface_rows, 0)

    def store_sens(half, i, x, y0, diff0):
        wide = yt + 8
        low, high = pl.ds(y0, wide), pl.ds(y0 + 1, wide)
        fy = face_of(jac, 1, [adj[k, x, low, :] for k in range(5)], [st[k, x, low, :] for k in range(5)],
                     [adj[k, x, high, :] for k in range(5)], [st[k, x, high, :] for k in range(5)])
        diff1 = fy[7:7 + yt] - fy[8:8 + yt]
        av, sv = cells(x, y0)
        fz = face_of(jac, 2, av, sv, [pltpu.roll(v, LANES - 1, 1) for v in av],
                     [pltpu.roll(v, LANES - 1, 1) for v in sv])
        edge = zface[pl.ds(y0, yt), :]
        z_hi = jnp.where(lane == LANES - 1, pltpu.roll(edge, LANES - 1 - 2 * x, 1), fz)
        z_lo = jnp.where(lane == 0, pltpu.roll(edge, LANES - 1 - 2 * x, 1), pltpu.roll(fz, 1, 1))
        diff2 = z_lo - z_hi
        ys = pl.ds(y0, yt)
        scaled = wing[x, ys, :].astype(F32) * sv[4]
        for c in range(3):
            value = scaled * sv[1 + c]
            value = value + met[0, c, x, ys, :] * diff0
            value = value + met[1, c, x, ys, :] * diff1
            value = value + met[2, c, x, ys, :] * diff2
            sens[half, i, c, ys, :] = value

    def chunk_of(t):
        return (a + 2 * nx - per * b - t) % nx

    def phase1(half, j):
        return remote(sens.at[half, :, :, pl.ds(pl.multiple_of(j * yt, yt), yt), :],
                      mid.at[half, a], s1.at[half, j], r1.at[half, a], (j, b))

    def own_chunk(half):
        return pltpu.make_async_copy(
            sens.at[half, :, :, pl.ds(pl.multiple_of(a * yt, yt), yt), :],
            mid.at[half, a], r1.at[half, a])

    def send_chunk(half, t):
        j = chunk_of(t)

        @pl.when(j != a)
        def _():
            phase1(half, j).start()

        @pl.when(j == a)
        def _():
            own_chunk(half).start()

    def slot(half, f, z):
        return recv.at[half, f % per, :, :, :, pl.ds(pl.multiple_of(z * LANES, LANES), LANES)]

    def phase2(half, f):
        return remote(mid.at[half, f], slot(half, f, b), s2.at[half, f], r2.at[half, f % per, b],
                      (a, f // per))

    def relay(half):
        def step(t, carry):
            f = (a + per * b + t) % nx
            remote(mid.at[half, f], mid.at[half, f], s1.at[half, f], r1.at[half, f], (f, b)).wait_recv()

            @pl.when(f // per != b)
            def _():
                phase2(half, f).start()

            @pl.when(f // per == b)
            def _():
                pltpu.make_async_copy(mid.at[half, f], slot(half, f, b), r2.at[half, f % per, b]).start()
            return carry

        lax.fori_loop(0, nx, step, 0)

    def make_half(half, compute):
        def step(t, carry):
            compute(pl.multiple_of(chunk_of(t) * yt, yt))

            @pl.when(t > 0)
            def _():
                send_chunk(half, t - 1)
            return carry

        lax.fori_loop(0, nx, step, 0)
        start_if(has_up, sp_up if half == 0 else [])
        start_if(has_dn, sp_dn if half == 0 else [])
        start_if(has_hi, sr_up if half == 0 else [])
        start_if(has_lo, sr_lo if half == 0 else [])
        send_chunk(half, nx - 1)

    def inner_planes(y0):
        for i, x in enumerate((1, 2)):
            store_sens(0, i, x, y0, fx[x - 1, pl.ds(y0, yt), :] - fx[x, pl.ds(y0, yt), :])

    make_half(0, inner_planes)
    relay(0)

    exchange_wait(has_hi, to_upper, has_lo, to_upper)
    exchange_wait(has_lo, to_lower, has_hi, to_lower)

    def bottom_rows(base):
        def step(n, carry):
            h0 = pl.multiple_of(n * yt, yt)
            ha, hs = cells(0, pl.multiple_of(h0 + base, yt))
            la = [halo[0, 0, k, pl.ds(h0, yt), :] for k in range(5)]
            ls = [halo[0, 1, k, pl.ds(h0, yt), :] for k in range(5)]
            xface[0, pl.ds(pl.multiple_of(h0 + base, yt), yt), :] = face_of(jac, 0, la, ls, ha, hs)
            return carry
        lax.fori_loop(0, half_y // yt, step, 0)

    def top_rows(base):
        def step(n, carry):
            h0 = pl.multiple_of(n * yt, yt)
            la, ls = cells(3, pl.multiple_of(h0 + base, yt))
            ha = [halo[1, 0, k, pl.ds(h0, yt), :] for k in range(5)]
            hs = [halo[1, 1, k, pl.ds(h0, yt), :] for k in range(5)]
            xface[1, pl.ds(pl.multiple_of(h0 + base, yt), yt), :] = face_of(jac, 0, la, ls, ha, hs)
            return carry
        lax.fori_loop(0, half_y // yt, step, 0)

    bottom_rows(0)
    top_rows(half_y)
    xf_lo = [remote(xface.at[0, first, :], xface.at[1, first, :], xf_s.at[0], xf_r.at[0], lower)]
    xf_up = [remote(xface.at[1, second, :], xface.at[0, second, :], xf_s.at[1], xf_r.at[1], upper)]
    start_if(has_lo, xf_lo)
    start_if(has_hi, xf_up)

    @pl.when(jnp.logical_not(has_lo))
    def _():
        bottom_rows(half_y)

    @pl.when(jnp.logical_not(has_hi))
    def _():
        top_rows(0)

    exchange_wait(has_lo, xf_lo, has_hi, xf_lo)
    exchange_wait(has_hi, xf_up, has_lo, xf_up)

    def outer_planes(y0):
        ys = pl.ds(y0, yt)
        store_sens(1, 0, 0, y0, xface[0, ys, :] - fx[0, ys, :])
        store_sens(1, 1, 3, y0, fx[2, ys, :] - xface[1, ys, :])

    make_half(1, outer_planes)

    exchange_wait(has_up, sp_up, has_dn, sp_up)
    exchange_wait(has_dn, sp_dn, has_up, sp_dn)
    exchange_wait(has_hi, sr_up, has_lo, sr_up)
    exchange_wait(has_lo, sr_lo, has_hi, sr_lo)
    relay(1)

    def put_rows(dst, src, side_row):
        dst[side_row:side_row + 1, :] = src

    def coup_plane(x, carry):
        stiff.at[x + 1][PAD - 1:PAD, :] = srow_in[0, pl.ds(x, 1), :]
        stiff.at[x + 1][PAD + yt:PAD + yt + 1, :] = srow_in[1, pl.ds(x, 1), :]
        zl = lax.broadcasted_iota(jnp.int32, (yt, span), 1)
        mid_s = stiff[x + 1, PAD:PAD + yt, :]
        around = [
            stiff[x + 2, PAD:PAD + yt, :],
            stiff[x, PAD:PAD + yt, :],
            stiff[x + 1, PAD + 1:PAD + 1 + yt, :],
            stiff[x + 1, PAD - 1:PAD - 1 + yt, :],
            jnp.where(zl == span - 1, 0.0, pltpu.roll(mid_s, span - 1, 1)),
            jnp.where(zl == 0, 0.0, pltpu.roll(mid_s, 1, 1)),
        ]
        faces = [0.5 * (mid_s + s) for s in around]
        diag = MASS + faces[0]
        for face in faces[1:]:
            diag = diag + face
        free = jnp.where(fix[x] == 0, 1.0, 0.0)
        weight = free * (RELAX / diag)
        wgt[x] = weight
        for n in range(4):
            coup[n, x] = weight * faces[n]
        coup[4, x] = jnp.where(zl == span - 1, 0.0, weight * faces[4])
        coup[5, x] = jnp.where(zl == 0, 0.0, weight * faces[5])
        return carry

    lax.fori_loop(0, xt, coup_plane, 0)

    def arrived(half):
        for h in range(per):
            for z in range(nz):
                dst = slot(half, h, z)
                remote(dst, dst, s2.at[half, 0], r2.at[half, h, z], (a, z)).wait_recv()

    def put_field(n, c, x, dst, value):
        dst[c, x + 1, PAD:PAD + yt, :] = value
        frow[n, 0, c, pl.ds(x, 1), :] = value[0:1]
        frow[n, 1, c, pl.ds(x, 1), :] = value[yt - 1:yt]

    for half, planes in enumerate(((1, 2), (0, 3))):
        arrived(half)

        def first_sweep(h, carry, half=half, planes=planes):
            for i, xl in enumerate(planes):
                x = h * 4 + xl
                for c in range(3):
                    put_field(0, c, x, field_a, wgt[x] * recv[half, h, i, c])
            return carry

        lax.fori_loop(0, per, first_sweep, 0)

    def exchange_field(n, field):
        p_up = [remote(field.at[:, xt, rows, :], field.at[:, 0, rows, :], fp_s.at[n, 0], fp_r.at[n, 0], above)]
        p_dn = [remote(field.at[:, 1, rows, :], field.at[:, xt + 1, rows, :], fp_s.at[n, 1], fp_r.at[n, 1], below)]
        r_up = [remote(frow.at[n, 1], frow_in.at[n, 0], fr_s.at[n, 0], fr_r.at[n, 0], upper)]
        r_lo = [remote(frow.at[n, 0], frow_in.at[n, 1], fr_s.at[n, 1], fr_r.at[n, 1], lower)]
        start_if(has_up, p_up)
        start_if(has_dn, p_dn)
        start_if(has_hi, r_up)
        start_if(has_lo, r_lo)
        return p_up, p_dn, r_up, r_lo

    def relaxed(n, field, x, store):
        for c in range(3):
            field.at[c, x + 1][PAD - 1:PAD, :] = frow_in[n, 0, c, pl.ds(x, 1), :]
            field.at[c, x + 1][PAD + yt:PAD + yt + 1, :] = frow_in[n, 1, c, pl.ds(x, 1), :]
            here = field[c, x + 1, PAD:PAD + yt, :]
            total = coup[0, x] * field[c, x + 2, PAD:PAD + yt, :]
            total = total + coup[1, x] * field[c, x, PAD:PAD + yt, :]
            total = total + coup[2, x] * field[c, x + 1, PAD + 1:PAD + 1 + yt, :]
            total = total + coup[3, x] * field[c, x + 1, PAD - 1:PAD - 1 + yt, :]
            total = total + coup[4, x] * pltpu.roll(here, span - 1, 1)
            total = total + coup[5, x] * pltpu.roll(here, 1, 1)
            start = here if n == 0 else field_a[c, x + 1, PAD:PAD + yt, :]
            store(c, x, (1.0 - RELAX) * here + start + total)

    def sweep(n, field, store):
        p_up, p_dn, r_up, r_lo = exchange_field(n, field)
        exchange_wait(has_hi, r_up, has_lo, r_up)
        exchange_wait(has_lo, r_lo, has_hi, r_lo)

        def step(x, carry):
            relaxed(n, field, x, store)
            return carry

        lax.fori_loop(1, xt - 1, step, 0)
        exchange_wait(has_up, p_up, has_dn, p_up)
        exchange_wait(has_dn, p_dn, has_up, p_dn)
        relaxed(n, field, 0, store)
        relaxed(n, field, xt - 1, store)

    def store_last(c, x, value):
        out[c, x] = value

    sweep(0, field_a, lambda c, x, value: put_field(1, c, x, field_b, value))
    sweep(1, field_b, store_last)

    for half in range(2):
        def drain(t, carry, half=half):
            @pl.when(t != a)
            def _():
                phase1(half, t).wait_send()

            @pl.when(t // per != b)
            def _():
                phase2(half, t).wait_send()
            return carry

        lax.fori_loop(0, nx, drain, 0)


def shards(nx, nz, adjoint, flow_state, jacobians, metric, wing_cells, modulus, stiff_class, fixed_cells):
    ny = adjoint.shape[2]
    xt, yt, span = modulus.shape
    per = nx // nz
    V, D = pltpu.VMEM, pltpu.SemaphoreType.DMA
    anywhere = pl.BlockSpec(memory_space=pl.ANY)
    scratch = [
        V((5, 4, ny + 2 * PAD, LANES), F32),
        V((5, 4, ny + 2 * PAD, LANES), F32),
        V(metric.shape, F32),
        V(wing_cells.shape, jnp.int32),
        V(modulus.shape, F32),
        V(modulus.shape, jnp.int32),
        V(modulus.shape, jnp.int32),
        V((2, 2, 5, ny // 2, LANES), F32),
        V((ny, LANES), F32),
        V((2, ny, LANES), F32),
        V((ny, LANES), F32),
        V((3, ny, LANES), F32),
        V((2, ny, LANES), F32),
        V((2, 2, 3, ny, LANES), F32),
        V((2, nx, 2, 3, yt, LANES), F32),
        V((2, per, 2, 3, yt, span), F32),
        V((xt + 2, yt + 2 * PAD, span), F32),
        V((2, xt, span), F32),
        V((2, xt, span), F32),
        V((xt, yt, span), F32),
        V((6, xt, yt, span), F32),
        V((3, xt + 2, yt + 2 * PAD, span), F32),
        V((3, xt + 2, yt + 2 * PAD, span), F32),
        V((2, 2, 3, xt, span), F32),
        V((2, 2, 3, xt, span), F32),
        D((7,)), D((2, 2)), D((2, 2)), D((2,)), D((2,)), D((2,)), D((2,)),
        D((2, nx)), D((2, nx)), D((2, nx)), D((2, per, nz)),
        D((2,)), D((2,)), D((2,)), D((2,)),
        D((2, 2)), D((2, 2)), D((2, 2)), D((2, 2)),
    ]
    return pl.pallas_call(
        functools.partial(kernel, nx, nz),
        out_shape=jax.ShapeDtypeStruct((3, xt, yt, span), F32),
        in_specs=[pl.BlockSpec(memory_space=pltpu.SMEM)] + [anywhere] * 7,
        out_specs=pl.BlockSpec(memory_space=pltpu.VMEM),
        scratch_shapes=scratch,
        compiler_params=pltpu.CompilerParams(
            collective_id=0, has_side_effects=True, vmem_limit_bytes=63 * 1024 * 1024),
        name="adjoint_step",
    )(jacobians, adjoint, flow_state, metric, wing_cells, modulus, stiff_class, fixed_cells)


def solution(mesh):
    return jax.shard_map(
        functools.partial(shards, mesh.shape["gx"], mesh.shape["gz"]),
        mesh=mesh,
        in_specs=(
            P(None, "gx", None, "gz"),
            P(None, "gx", None, "gz"),
            P(),
            P(None, None, "gx", None, "gz"),
            P("gx", None, "gz"),
            P("gz", "gx", None),
            P("gz", "gx", None),
            P("gz", "gx", None),
        ),
        out_specs=P(None, "gz", "gx", None),
        check_vma=False,
    )
```
